32 devices in a mesh: batch: 2 (over y), fsdp: 16 (over z, x, core).
Axes of the slice: x: 2, y: 2, z: 4, core: 2. Of those that a mesh axis runs over, the one named last changes fastest.
Arguments:
- trunk: bfloat16 [6144, 4096], P('fsdp', 'batch'), may hold values from -0.75 to 0.75
- pre_act: bfloat16 [4096, 1024], P(('batch', 'fsdp')), may hold values from -6 to 6
- proj_weight: bfloat16 [6144, 1024], P('fsdp'), may hold values from -0.1875 to 0.1875
- codebook: bfloat16 [2048, 1024], P('fsdp'), may hold values from -1.6 to 1.6
- value_weight: bfloat16 [1024, 601], P('fsdp'), may hold values from -1.6 to 1.6
- code_target: int32 [4096], P(('batch', 'fsdp')), may hold values from 0 to 2047
- value_bin: int32 [4096], P(('batch', 'fsdp')), may hold values from 0 to 599
- value_frac: int32 [4096], P(('batch', 'fsdp')), may hold values from 0 to 1024
Outputs:
- grad_trunk: bfloat16 [6144, 4096], P('fsdp', 'batch')
- grad_proj: float32 [6144, 1024], P('fsdp')
- grad_codebook: float32 [2048, 1024], P('fsdp')
- grad_value: float32 [1024, 601], P('fsdp')
The draws below stay inside these ranges and needn't reach their ends.
All inputs are finite; a program needn't handle non-finite values.
Results may differ from the reference program's by a relative error of at most 0.012.
Values may be sent and summed in bfloat16 or wider, within the bound.
A program may use at most 64 MiB of HBM per device.

```python
import math
import jax
import jax.numpy as jnp
from jax import lax

WIDTH = 6144
CODE_DIM = 1024
CODES = 2048
BINS = 601
ROWS_DEV = 128
POSITIONS = 4096
N_BATCH = 2
N_FSDP = 16


def draw_pre_act(key, part):
    entries = jnp.clip(jax.random.normal(jax.random.fold_in(key, 4), (POSITIONS, CODE_DIM), jnp.float32), -6.0, 6.0)
    return entries.astype(jnp.bfloat16)


def draw_codebook(key, part):
    spread = 5.0 / math.sqrt(CODE_DIM)
    entries = jnp.clip(jax.random.normal(jax.random.fold_in(key, 6), (CODES, CODE_DIM), jnp.float32), -4.0, 4.0) * spread
    return entries.astype(jnp.bfloat16)


def draw_value_weight(key, part):
    spread = 5.0 / math.sqrt(CODE_DIM)
    entries = jnp.clip(jax.random.normal(jax.random.fold_in(key, 9), (CODE_DIM, BINS), jnp.float32), -4.0, 4.0) * spread
    return entries.astype(jnp.bfloat16)


def place_ends(drawn, key, low, high):
    spot = [jax.random.randint(jax.random.fold_in(key, axis), (), 0, length) for axis, length in enumerate(drawn.shape)]
    longest = drawn.shape.index(max(drawn.shape))
    beside = spot[:longest] + [(spot[longest] + 1) % drawn.shape[longest]] + spot[longest + 1:]
    return drawn.at[tuple(spot)].set(low).at[tuple(beside)].set(high)


def shard_levels(stream_key, shape, split, least, high):
    factor_of = 1.0
    for axis_at, shards_of in split:
        heights = jax.random.uniform(jax.random.fold_in(jax.random.fold_in(stream_key, 6), axis_at), (shards_of,), jnp.float32, least / len(split), high / len(split))
        factor_of = factor_of * jnp.repeat(jnp.exp(heights), shape[axis_at] // shards_of).reshape((-1,) + (1,) * (len(shape) - 1 - axis_at))
    return factor_of


def normal_values(own_key, extent, scale, reach, shards=(), kind=jnp.bfloat16):
    values = jax.random.normal(own_key, extent, jnp.float32) * scale
    if len(shards) > 0:
        values = shard_levels(own_key, extent, shards, -0.22, 0.18) * values
    return jnp.clip(values, min=-reach, max=reach).astype(kind)


def setup_inputs(seed: int = 0) -> dict:
    key_of = jax.random.split(jax.random.key(seed), 9)
    trunk = normal_values(key_of[0], (WIDTH, POSITIONS), 0.05, 0.75, ((0, 16), (1, 2)))
    pre_act = draw_pre_act(jax.random.fold_in(key_of[8], 71), 0)
    proj_weight = normal_values(key_of[2], (WIDTH, CODE_DIM), CODE_DIM ** -0.5, 0.1875, ((0, 16),))
    codebook = draw_codebook(jax.random.fold_in(key_of[8], 71), 0)
    value_weight = draw_value_weight(jax.random.fold_in(key_of[8], 71), 0)
    code_target = place_ends(jax.random.randint(key_of[5], (POSITIONS,), 0, CODES), jax.random.fold_in(key_of[5], 1), 0, CODES - 1).astype(jnp.int32)
    value_bin = place_ends(jax.random.randint(key_of[6], (POSITIONS,), 0, BINS - 1), jax.random.fold_in(key_of[6], 1), 0, (BINS - 1) - 1).astype(jnp.int32)
    value_frac = place_ends(jax.random.randint(key_of[7], (POSITIONS,), 0, 1025), jax.random.fold_in(key_of[7], 1), 0, 1024).astype(jnp.int32)
    return dict(trunk=trunk, pre_act=pre_act, proj_weight=proj_weight, codebook=codebook, value_weight=value_weight, code_target=code_target, value_bin=value_bin, value_frac=value_frac)


def reference(trunk, pre_act, proj_weight, codebook, value_weight, code_target, value_bin, value_frac):
    block_rows = ROWS_DEV * N_FSDP
    trunk_blocks = trunk.reshape(WIDTH, N_BATCH, block_rows).transpose(1, 0, 2)
    pre_blocks = pre_act.reshape(N_BATCH, block_rows, CODE_DIM)
    code_blocks = code_target.reshape(N_BATCH, block_rows)
    bin_blocks = value_bin.reshape(N_BATCH, block_rows)
    frac_blocks = value_frac.reshape(N_BATCH, block_rows)
    code_ids = jnp.arange(CODES, dtype=jnp.int32)[None, :]
    bin_ids = jnp.arange(BINS, dtype=jnp.int32)[None, :]

    def block_step(totals, inputs):
        proj_total, code_total, value_total = totals
        trunk_cols, pre_rows, code_rows, bin_rows, frac_rows = inputs
        pre_value = pre_rows.astype(jnp.float32)
        gate_sigma = jax.nn.sigmoid(pre_value)
        active = (pre_value * gate_sigma).astype(jnp.bfloat16)
        code_logits = jnp.dot(active, codebook.T, preferred_element_type=jnp.float32)
        code_probs = jax.nn.softmax(code_logits, axis=-1)
        one_hot = (code_rows[:, None] == code_ids).astype(jnp.float32)
        code_delta = (code_probs - one_hot).astype(jnp.bfloat16)
        value_logits = jnp.dot(active, value_weight, preferred_element_type=jnp.float32)
        value_probs = jax.nn.softmax(value_logits, axis=-1)
        fraction = frac_rows.astype(jnp.float32)[:, None] / 1024.0
        target = jnp.where(bin_ids == bin_rows[:, None], 1.0 - fraction, 0.0)
        target = target + jnp.where(bin_ids == bin_rows[:, None] + 1, fraction, 0.0)
        value_delta = (value_probs - target).astype(jnp.bfloat16)
        backward = jnp.dot(code_delta, codebook, preferred_element_type=jnp.float32)
        backward = backward + jnp.dot(value_delta, value_weight.T, preferred_element_type=jnp.float32)
        pre_grad = (backward * gate_sigma * (1.0 + pre_value * (1.0 - gate_sigma))).astype(jnp.bfloat16)
        code_total = code_total + jnp.dot(code_delta.T, active, preferred_element_type=jnp.float32)
        value_total = value_total + jnp.dot(active.T, value_delta, preferred_element_type=jnp.float32)
        proj_total = proj_total + jnp.dot(trunk_cols, pre_grad, preferred_element_type=jnp.float32)
        trunk_grad = jnp.dot(proj_weight, pre_grad.T, preferred_element_type=jnp.float32).astype(jnp.bfloat16)
        return (proj_total, code_total, value_total), trunk_grad

    initial = (jnp.zeros((WIDTH, CODE_DIM), jnp.float32), jnp.zeros((CODES, CODE_DIM), jnp.float32), jnp.zeros((CODE_DIM, BINS), jnp.float32))
    totals, trunk_grads = lax.scan(block_step, initial, (trunk_blocks, pre_blocks, code_blocks, bin_blocks, frac_blocks))
    return trunk_grads.transpose(1, 0, 2).reshape(WIDTH, POSITIONS), totals[0], totals[1], totals[2]
```

```python
import jax
import jax.numpy as jnp
from jax import lax
from jax.experimental import pallas as pl
from jax.experimental.pallas import tpu as pltpu
from jax.sharding import PartitionSpec as P

MESH = pl.DeviceIdType.MESH
BF16 = jnp.bfloat16
F32 = jnp.float32
CORES = 2
PLANES = 4


class Place:
    def __init__(self, nb, nf):
        self.nb, self.nz = nb, PLANES
        self.nx = nf // (PLANES * CORES)
        f = lax.axis_index("fsdp")
        self.b = lax.axis_index("batch")
        self.z = f // (self.nx * CORES)
        self.x = (f // CORES) % self.nx
        self.c = f % CORES

    def dev(self, b=None, z=None, x=None, c=None):
        b = self.b if b is None else b
        z = self.z if z is None else z
        x = self.x if x is None else x
        c = self.c if c is None else c
        return (b, (z * self.nx + x) * CORES + c)

    def zz(self, d):
        return lax.rem(self.z + d + self.nz, self.nz)

    def xx(self, d):
        return lax.rem(self.x + d + self.nx, self.nx)

    def bb(self, d):
        return lax.rem(self.b + d + self.nb, self.nb)

    def barrier(self):
        sem = pltpu.get_barrier_semaphore()
        peers = [self.dev(z=self.zz(d)) for d in range(1, self.nz)]
        peers += [self.dev(x=self.xx(d)) for d in range(1, self.nx)]
        peers += [self.dev(b=self.bb(d)) for d in range(1, self.nb)]
        peers += [self.dev(c=1 - self.c)]
        for peer in peers:
            pl.semaphore_signal(sem, inc=1, device_id=peer, device_id_type=MESH)
        pl.semaphore_wait(sem, len(peers))


class Sends:
    def __init__(self, send_sem, recv_sem, keys):
        self.send_sem, self.recv_sem = send_sem, recv_sem
        self.at = {k: i for i, k in enumerate(keys)}
        self.started = []
        self.pending = {}

    def go(self, key, src, dst, dev):
        i = self.at[key]
        copy = pltpu.make_async_remote_copy(
            src_ref=src,
            dst_ref=dst,
            send_sem=self.send_sem.at[i],
            recv_sem=self.recv_sem.at[i],
            device_id=dev,
            device_id_type=MESH,
        )
        copy.start()
        self.started.append(copy)
        self.pending[key] = copy

    def arrived(self, key):
        self.pending[key].wait_recv()

    def finish(self):
        for copy in self.started:
            copy.wait_send()


def call(kernel, outs, scratch, cid, *args):
    return pl.pallas_call(
        kernel,
        out_shape=outs,
        in_specs=[pl.BlockSpec(memory_space=pltpu.VMEM)] * len(args),
        out_specs=[pl.BlockSpec(memory_space=pltpu.VMEM)] * len(outs),
        scratch_shapes=scratch,
        compiler_params=pltpu.CompilerParams(collective_id=cid, has_side_effects=True),
    )(*args)


def gather_weights_keys(nb, nx, nz):
    keys = []
    for a in (0, 1):
        keys += [(a, "c", 0)]
        for dz in range(nz):
            if dz:
                keys += [(a, "z", dz), (a, "cz", dz)]
                for dy in range(1, nb):
                    keys += [(a, "y", dz, dy), (a, "cy", dz, dy)]
            for dx in range(1, nx):
                keys += [(a, "x", dz, dx), (a, "cx", dz, dx)]
                for dy in range(1, nb):
                    keys += [(a, "d", dz, dx, dy), (a, "cd", dz, dx, dy)]
    return keys


def gather_weights(nb, nf, codebook, value_weight):
    nz, nx = PLANES, nf // (PLANES * CORES)
    keys = gather_weights_keys(nb, nx, nz)
    rows, width = codebook.shape
    vrows, bins = value_weight.shape

    def kernel(cb, vw, cb_out, vw_out, send_sem, recv_sem):
        p = Place(nb, nf)
        p.barrier()
        s = Sends(send_sem, recv_sem, keys)
        arrays = ((0, cb, cb_out), (1, vw, vw_out))

        def spot(out, z, x, h):
            return out.at[z, x, p.c, h]

        def relay(key, out, at_z, at_x, at_h, **to):
            ref = spot(out, at_z, at_x, at_h)
            s.go(key, ref, ref, p.dev(**to))

        for a, own, out in arrays:
            here = spot(out, p.z, p.x, p.b)
            for dz in range(1, nz):
                s.go((a, "z", dz), own.at[p.b], here, p.dev(z=p.zz(dz)))
            for dx in range(1, nx):
                s.go((a, "x", 0, dx), own.at[p.b], here, p.dev(x=p.xx(dx)))
            s.go((a, "c", 0), own, out.at[p.z, p.x, p.c], p.dev(c=1 - p.c))
        for a, own, out in arrays:
            out[p.z, p.x, p.c] = own[...]
        for dz in range(nz + 1):
            for a, own, out in arrays:
                if 1 <= dz < nz:
                    z = p.zz(-dz)
                    s.arrived((a, "z", dz))
                    for dx in range(1, nx):
                        relay((a, "x", dz, dx), out, z, p.x, p.b, x=p.xx(dx))
                    for dy in range(1, nb):
                        relay((a, "y", dz, dy), out, z, p.x, p.b, b=p.bb(dy))
                    relay((a, "cz", dz), out, z, p.x, p.b, c=1 - p.c)
            e = dz - 1
            if e < 0:
                continue
            for a, own, out in arrays:
                z = p.zz(-e)
                for dx in range(1, nx):
                    x = p.xx(-dx)
                    s.arrived((a, "x", e, dx))
                    if e % 2 == 0:
                        for dy in range(1, nb):
                            relay((a, "d", e, dx, dy), out, z, x, p.b, b=p.bb(dy))
                    relay((a, "cx", e, dx), out, z, x, p.b, c=1 - p.c)
                if e:
                    for dy in range(1, nb):
                        h = p.bb(-dy)
                        s.arrived((a, "y", e, dy))
                        if e % 2:
                            for dx in range(1, nx):
                                relay((a, "d", e, dx, dy), out, z, p.x, h, x=p.xx(dx))
                        relay((a, "cy", e, dy), out, z, p.x, h, c=1 - p.c)
        for e in range(nz):
            for a, own, out in arrays:
                for dx in range(1, nx):
                    for dy in range(1, nb):
                        s.arrived((a, "d", e, dx, dy))
                        relay(
                            (a, "cd", e, dx, dy), out, p.zz(-e), p.xx(-dx), p.bb(-dy), c=1 - p.c
                        )
        for key in keys:
            if key[1][0] == "c":
                s.arrived(key)
        s.finish()

    cb_out, vw_out = call(
        kernel,
        [
            jax.ShapeDtypeStruct((nz, nx, CORES, nb, rows // nb, width), BF16),
            jax.ShapeDtypeStruct((nz, nx, CORES, nb, vrows // nb, bins), BF16),
        ],
        [pltpu.SemaphoreType.DMA((len(keys),)), pltpu.SemaphoreType.DMA((len(keys),))],
        1,
        codebook.reshape(nb, rows // nb, width),
        value_weight.reshape(nb, vrows // nb, bins),
    )
    return cb_out.reshape(nf * rows, width), vw_out.reshape(nf * vrows, bins)


def gather_grads(nb, nf, pre_grad, active, delta_t, value_delta):
    nz, nx = PLANES, nf // (PLANES * CORES)
    rows, width = pre_grad.shape
    bins = value_delta.shape[1]
    half = delta_t.shape[1]
    keys = [("c", 0)]
    for dz in range(nz):
        if dz:
            keys += [("z", dz), ("cz", dz)]
        for dx in range(1, nx):
            keys += [("x", dz, dx), ("cx", dz, dx)]
    keys += [(k, dy) for dy in range(1, nb) for k in ("act", "delta", "value")]

    def kernel(pg, act, dt, vd, pg_out, act_out, dt_out, vd_out, send_sem, recv_sem):
        p = Place(nb, nf)
        p.barrier()
        s = Sends(send_sem, recv_sem, keys)
        here = pg_out.at[p.z, p.x, p.c]
        for dz in range(1, nz):
            s.go(("z", dz), pg, here, p.dev(z=p.zz(dz)))
        for dx in range(1, nx):
            s.go(("x", 0, dx), pg, here, p.dev(x=p.xx(dx)))
        for dy in range(1, nb):
            to = p.bb(dy)
            s.go(("act", dy), act, act_out.at[p.b], p.dev(b=to))
            s.go(("delta", dy), dt.at[to], dt_out.at[p.b], p.dev(b=to))
            s.go(("value", dy), vd, vd_out.at[p.b], p.dev(b=to))
        s.go(("c", 0), pg, here, p.dev(c=1 - p.c))
        pg_out[p.z, p.x, p.c] = pg[...]
        act_out[p.b] = act[...]
        dt_out[p.b] = dt[p.b]
        vd_out[p.b] = vd[...]
        for dz in range(nz + 1):
            if 1 <= dz < nz:
                s.arrived(("z", dz))
                ref = pg_out.at[p.zz(-dz), p.x, p.c]
                for dx in range(1, nx):
                    s.go(("x", dz, dx), ref, ref, p.dev(x=p.xx(dx)))
                s.go(("cz", dz), ref, ref, p.dev(c=1 - p.c))
            if dz:
                e = dz - 1
                for dx in range(1, nx):
                    s.arrived(("x", e, dx))
                    ref = pg_out.at[p.zz(-e), p.xx(-dx), p.c]
                    s.go(("cx", e, dx), ref, ref, p.dev(c=1 - p.c))
        for key in keys:
            if key[0] not in ("x", "z"):
                s.arrived(key)
        s.finish()

    pieces, act_all, dt_all, vd_all = call(
        kernel,
        [
            jax.ShapeDtypeStruct((nz, nx, CORES, rows, width), BF16),
            jax.ShapeDtypeStruct((nb, rows, width), BF16),
            jax.ShapeDtypeStruct((nb, half, rows), BF16),
            jax.ShapeDtypeStruct((nb, rows, bins), BF16),
        ],
        [pltpu.SemaphoreType.DMA((len(keys),)), pltpu.SemaphoreType.DMA((len(keys),))],
        2,
        pre_grad,
        active,
        delta_t,
        value_delta,
    )
    return pieces.reshape(nf * rows, width), act_all, dt_all, vd_all


def reduce_grads(nb, nf, proj, code, value):
    nz, nx = PLANES, nf // (PLANES * CORES)
    keys = [("p", dy) for dy in range(1, nb)]
    for a in (0, 1):
        keys += [(a, "c")] + [(a, "x", d) for d in range(1, nx)]
        keys += [(a, "z", d) for d in range(1, nz)] + [(a, "y", d) for d in range(1, nb)]

    def kernel(pj, cd, vl, pj_out, cd_out, vl_out, pj_in, *rest):
        (cc, cx, cxs, cacc, cz, czs, cy, vc, vx, vxs, vacc, vz, vzs, vy) = rest[:14]
        send_sem, recv_sem = rest[14:]
        p = Place(nb, nf)
        p.barrier()
        s = Sends(send_sem, recv_sem, keys)
        arrays = (
            (0, cd, cd_out, cc, cx, cxs, cacc, cz, czs, cy),
            (1, vl, vl_out, vc, vx, vxs, vacc, vz, vzs, vy),
        )
        for a, own, out, core, *_ in arrays:
            s.go((a, "c"), own.at[1 - p.c], core, p.dev(c=1 - p.c))
        for dy in range(1, nb):
            s.go(("p", dy), pj, pj_in.at[p.b], p.dev(b=p.bb(dy)))
        for a, own, out, core, xin, xsend, acc, zin, zsend, yall in arrays:
            s.arrived((a, "c"))
            for dx in range(1, nx):
                x = p.xx(dx)
                xsend[dx - 1] = (own[p.c, x].astype(F32) + core[x].astype(F32)).astype(BF16)
                s.go((a, "x", dx), xsend.at[dx - 1], xin.at[dx - 1], p.dev(x=x))
            acc[...] = own[p.c, p.x].astype(F32) + core[p.x].astype(F32)
        for a, own, out, core, xin, xsend, acc, zin, zsend, yall in arrays:
            for dx in range(1, nx):
                s.arrived((a, "x", dx))
                acc[...] += xin[dx - 1].astype(F32)
            for dz in (2, 1, 3):
                z = p.zz(dz)
                zsend[dz - 1] = acc[z].astype(BF16)
                s.go((a, "z", dz), zsend.at[dz - 1], zin.at[dz - 1], p.dev(z=z))
        for a, own, out, core, xin, xsend, acc, zin, zsend, yall in arrays:
            total = acc[p.z]
            for dz in range(1, nz):
                s.arrived((a, "z", dz))
                total = total + zin[dz - 1].astype(F32)
            yall[p.b] = total.astype(BF16)
            for dy in range(1, nb):
                s.go((a, "y", dy), yall.at[p.b], yall.at[p.b], p.dev(b=p.bb(dy)))
        for dy in range(1, nb):
            s.arrived(("p", dy))
        pj_in[p.b] = pj[...]
        total = pj_in[0].astype(F32)
        for h in range(1, nb):
            total = total + pj_in[h].astype(F32)
        pj_out[...] = total
        for a, own, out, core, xin, xsend, acc, zin, zsend, yall in arrays:
            for dy in range(1, nb):
                s.arrived((a, "y", dy))
            out[...] = yall[...].astype(F32)
        s.finish()

    def buffers(part):
        r, k = part
        return [
            pltpu.VMEM((nx, nz, r, k), BF16),
            pltpu.VMEM((max(nx - 1, 1), nz, r, k), BF16),
            pltpu.VMEM((max(nx - 1, 1), nz, r, k), BF16),
            pltpu.VMEM((nz, r, k), F32),
            pltpu.VMEM((nz - 1, r, k), BF16),
            pltpu.VMEM((nz - 1, r, k), BF16),
            pltpu.VMEM((nb, r, k), BF16),
        ]

    outs = [
        jax.ShapeDtypeStruct(proj.shape, F32),
        jax.ShapeDtypeStruct((nb,) + code.shape[3:], F32),
        jax.ShapeDtypeStruct((nb,) + value.shape[3:], F32),
    ]
    proj_sum, code_sum, value_sum = call(
        kernel,
        outs,
        [pltpu.VMEM((nb,) + proj.shape, BF16)]
        + buffers(code.shape[3:])
        + buffers(value.shape[3:])
        + [pltpu.SemaphoreType.DMA((len(keys),)), pltpu.SemaphoreType.DMA((len(keys),))],
        3,
        proj,
        code,
        value,
    )
    return (
        proj_sum,
        code_sum.reshape(-1, code.shape[-1]),
        value_sum.reshape(-1, value.shape[-1]),
    )


def make_body(nb, nf):
    nz, nx = PLANES, nf // (PLANES * CORES)

    def body(
        trunk, pre_act, proj_weight, codebook, value_weight, code_target, value_bin, value_frac
    ):
        me_b = lax.axis_index("batch")
        all_codes, bins_weight = gather_weights(nb, nf, codebook, value_weight)
        rows, width = pre_act.shape
        num_codes = all_codes.shape[0]
        num_bins = bins_weight.shape[1]
        pre_value = pre_act.astype(F32)
        gate_sigma = jax.nn.sigmoid(pre_value)
        active = (pre_value * gate_sigma).astype(BF16)
        code_logits = jnp.einsum("rk,ck->rc", active, all_codes, preferred_element_type=F32)
        code_probs = jax.nn.softmax(code_logits, axis=-1)
        code_ids = lax.broadcasted_iota(jnp.int32, (1, num_codes), 1)
        one_hot = (code_target[:, None] == code_ids).astype(F32)
        code_delta = (code_probs - one_hot).astype(BF16)
        value_logits = jnp.dot(active, bins_weight, preferred_element_type=F32)
        value_probs = jax.nn.softmax(value_logits, axis=-1)
        bin_ids = lax.broadcasted_iota(jnp.int32, (1, num_bins), 1)
        fraction = value_frac.astype(F32)[:, None] / 1024.0
        target = jnp.where(bin_ids == value_bin[:, None], 1.0 - fraction, 0.0)
        target = target + jnp.where(bin_ids == value_bin[:, None] + 1, fraction, 0.0)
        value_delta = (value_probs - target).astype(BF16)
        backward = jnp.dot(code_delta, all_codes, preferred_element_type=F32)
        backward = backward + jnp.einsum(
            "rb,kb->rk", value_delta, bins_weight, preferred_element_type=F32
        )
        pre_grad = (backward * gate_sigma * (1.0 + pre_value * (1.0 - gate_sigma))).astype(BF16)
        own = codebook.shape[0] // nb
        delta_t = code_delta.T.reshape(nf, nb, own, rows).swapaxes(0, 1)
        delta_t = delta_t.reshape(nb, nf * own, rows)
        pieces, act_all, dt_all, vd_all = gather_grads(
            nb, nf, pre_grad, active, delta_t, value_delta
        )
        weight_total = jnp.einsum("dr,rk->dk", trunk, pieces, preferred_element_type=F32)
        out_cols = jnp.einsum(
            "dk,rk->dr", proj_weight, pieces, preferred_element_type=F32
        ).astype(BF16)
        code_part = jnp.einsum("ncr,nrk->ck", dt_all, act_all, preferred_element_type=F32)
        code_part = code_part.astype(BF16).reshape(nz, nx, CORES, own, width)
        value_part = jnp.einsum("nrk,nrb->kb", act_all, vd_all, preferred_element_type=F32)
        vown = value_weight.shape[0] // nb
        value_part = value_part.astype(BF16).reshape(nz, nx, CORES, nb, vown, num_bins)
        value_part = lax.dynamic_index_in_dim(value_part, me_b, 3, keepdims=False)
        order = (2, 1, 0, 3, 4)
        proj_grad, code_grad, value_grad = reduce_grads(
            nb,
            nf,
            weight_total.astype(BF16),
            code_part.transpose(order),
            value_part.transpose(order),
        )
        return (out_cols, proj_grad, code_grad, value_grad)

    return body


def solution(mesh):
    in_specs = (
        P("fsdp", "batch"),
        P(("batch", "fsdp"), None),
        P("fsdp", None),
        P("fsdp", None),
        P("fsdp", None),
        P(("batch", "fsdp")),
        P(("batch", "fsdp")),
        P(("batch", "fsdp")),
    )
    out_specs = (P("fsdp", "batch"), P("fsdp", None), P("fsdp", None), P("fsdp", None))
    body = make_body(mesh.shape["batch"], mesh.shape["fsdp"])
    return jax.shard_map(body, mesh=mesh, in_specs=in_specs, out_specs=out_specs, check_vma=False)
```

```python
import jax
import jax.numpy as jnp
from jax import lax
from jax.experimental import pallas as pl
from jax.experimental.pallas import tpu as pltpu
from jax.sharding import PartitionSpec as P

MESH = pl.DeviceIdType.MESH
BF16 = jnp.bfloat16
F32 = jnp.float32
CORES = 2
PLANES = 4


class Place:
    def __init__(self, nb, nf):
        self.nb, self.nz = nb, PLANES
        self.nx = nf // (PLANES * CORES)
        f = lax.axis_index("fsdp")
        self.b = lax.axis_index("batch")
        self.z = f // (self.nx * CORES)
        self.x = (f // CORES) % self.nx
        self.c = f % CORES

    def dev(self, b=None, z=None, x=None, c=None):
        b = self.b if b is None else b
        z = self.z if z is None else z
        x = self.x if x is None else x
        c = self.c if c is None else c
        return (b, (z * self.nx + x) * CORES + c)

    def zz(self, d):
        return lax.rem(self.z + d + self.nz, self.nz)

    def xx(self, d):
        return lax.rem(self.x + d + self.nx, self.nx)

    def bb(self, d):
        return lax.rem(self.b + d + self.nb, self.nb)

    def barrier(self):
        sem = pltpu.get_barrier_semaphore()
        peers = [self.dev(z=self.zz(d)) for d in range(1, self.nz)]
        peers += [self.dev(x=self.xx(d)) for d in range(1, self.nx)]
        peers += [self.dev(b=self.bb(d)) for d in range(1, self.nb)]
        peers += [self.dev(c=1 - self.c)]
        for peer in peers:
            pl.semaphore_signal(sem, inc=1, device_id=peer, device_id_type=MESH)
        pl.semaphore_wait(sem, len(peers))


def steps(nz):
    return [(way, far) for far in range(1, nz) for way in (1, -1)]


class Sends:
    def __init__(self, send_sem, recv_sem, keys, place):
        self.send_sem, self.recv_sem, self.place = send_sem, recv_sem, place
        self.at = {k: i for i, k in enumerate(keys)}
        self.like = {}
        self.started = []
        self.when = ()

    def make(self, key, src, dst, dev):
        i = self.at[key]
        return pltpu.make_async_remote_copy(
            src_ref=src,
            dst_ref=dst,
            send_sem=self.send_sem.at[i],
            recv_sem=self.recv_sem.at[i],
            device_id=dev,
            device_id_type=MESH,
        )

    def go(self, key, src, dst, dev, like=None):
        self.make(key, src, dst, dev).start()
        self.like[key] = dst if like is None else like
        self.started.append((key, self.when))

    def waiter(self, key):
        ref = self.like[key]
        ref = ref() if callable(ref) else ref
        return self.make(key, ref, ref, self.place.dev(c=1 - self.place.c))

    def arrived(self, key):
        self.waiter(key).wait_recv()

    def finish(self):
        for key, whens in self.started:

            def wait(key=key):
                self.waiter(key).wait_send()

            if whens:
                met = whens[0]()
                for when in whens[1:]:
                    met = jnp.logical_and(met, when())
                pl.when(met)(wait)
            else:
                wait()

    def only(self, when):
        def run(f):
            outer = self.when
            self.when = outer + (when,)

            @pl.when(when())
            def _():
                f()

            self.when = outer

        return run


def call(kernel, outs, scratch, cid, *args):
    return pl.pallas_call(
        kernel,
        out_shape=outs,
        in_specs=[pl.BlockSpec(memory_space=pltpu.VMEM)] * len(args),
        out_specs=[pl.BlockSpec(memory_space=pltpu.VMEM)] * len(outs),
        scratch_shapes=scratch,
        compiler_params=pltpu.CompilerParams(collective_id=cid, has_side_effects=True),
    )(*args)


def has(p, way, far):
    return p.z >= far if way == 1 else p.z + far < p.nz


def feeds(p, way):
    return p.z + 1 < p.nz if way == 1 else p.z >= 1


def gather_weights_keys(nb, nx, nz):
    keys = []
    for a in (0, 1):
        keys += [(a, "c", 0)]
        for hop in [(0, 0)] + steps(nz):
            if hop[1]:
                keys += [(a, "z", hop), (a, "cz", hop)]
                for dy in range(1, nb):
                    keys += [(a, "y", hop, dy), (a, "cy", hop, dy)]
            for dx in range(1, nx):
                keys += [(a, "x", hop, dx), (a, "cx", hop, dx)]
                for dy in range(1, nb):
                    keys += [(a, "d", hop, dx, dy), (a, "cd", hop, dx, dy)]
    return keys


def gather_weights(nb, nf, codebook, value_weight):
    nz, nx = PLANES, nf // (PLANES * CORES)
    keys = gather_weights_keys(nb, nx, nz)
    rows, width = codebook.shape
    vrows, bins = value_weight.shape

    def kernel(cb, vw, cb_out, vw_out, send_sem, recv_sem):
        p = Place(nb, nf)
        p.barrier()
        s = Sends(send_sem, recv_sem, keys, p)
        arrays = ((0, cb, cb_out), (1, vw, vw_out))

        def spot(out, z, x, h):
            return out.at[z, x, p.c, h]

        def relay(key, out, at_z, at_x, at_h, **to):
            ref = spot(out, at_z, at_x, at_h)
            s.go(key, ref, ref, p.dev(**to), lambda: out.at[0, 0, 0, 0])

        for a, own, out in arrays:
            here = spot(out, p.z, p.x, p.b)
            for way in (1, -1):

                @s.only(lambda way=way: feeds(p, way))
                def _(a=a, own=own, out=out, here=here, way=way):
                    s.go((a, "z", (way, 1)), own.at[p.b], here, p.dev(z=p.z + way), lambda: out.at[0, 0, 0, 0])

            for dx in range(1, nx):
                s.go((a, "x", (0, 0), dx), own.at[p.b], here, p.dev(x=p.xx(dx)))
            s.go((a, "c", 0), own, out.at[p.z, p.x, p.c], p.dev(c=1 - p.c))
        for a, own, out in arrays:
            out[p.z, p.x, p.c] = own[...]

        def from_z(hop):
            way, far = hop
            z = p.z - way * far
            for a, own, out in arrays:
                s.arrived((a, "z", hop))
                if far + 1 < nz:

                    @s.only(lambda way=way: feeds(p, way))
                    def _(a=a, out=out):
                        relay((a, "z", (way, far + 1)), out, z, p.x, p.b, z=p.z + way)

                for dx in range(1, nx):
                    relay((a, "x", hop, dx), out, z, p.x, p.b, x=p.xx(dx))
                for dy in range(1, nb):
                    relay((a, "y", hop, dy), out, z, p.x, p.b, b=p.bb(dy))
                relay((a, "cz", hop), out, z, p.x, p.b, c=1 - p.c)

        def from_plane(hop):
            way, far = hop
            z = p.z - way * far
            for a, own, out in arrays:
                for dx in range(1, nx):
                    x = p.xx(-dx)
                    s.arrived((a, "x", hop, dx))
                    if far % 2 == 0:
                        for dy in range(1, nb):
                            relay((a, "d", hop, dx, dy), out, z, x, p.b, b=p.bb(dy))
                    relay((a, "cx", hop, dx), out, z, x, p.b, c=1 - p.c)
                if far:
                    for dy in range(1, nb):
                        h = p.bb(-dy)
                        s.arrived((a, "y", hop, dy))
                        if far % 2:
                            for dx in range(1, nx):
                                relay((a, "d", hop, dx, dy), out, z, p.x, h, x=p.xx(dx))
                        relay((a, "cy", hop, dy), out, z, p.x, h, c=1 - p.c)

        def from_diagonal(hop):
            way, far = hop
            for a, own, out in arrays:
                for dx in range(1, nx):
                    for dy in range(1, nb):
                        s.arrived((a, "d", hop, dx, dy))
                        relay(
                            (a, "cd", hop, dx, dy),
                            out,
                            p.z - way * far,
                            p.xx(-dx),
                            p.bb(-dy),
                            c=1 - p.c,
                        )

        def from_core(hop):
            for key in keys:
                if key[1] in ("cz", "cx", "cy", "cd") and key[2] == hop:
                    s.arrived(key)

        def under(hop, f):
            if hop[1]:
                s.only(lambda: has(p, *hop))(lambda: f(hop))
            else:
                f(hop)

        hops = [(0, 0)] + steps(nz)
        by_far = [[h for h in hops if h[1] == far] for far in range(nz)]
        for far in range(nz + 2):
            if 1 <= far < nz:
                for hop in by_far[far]:
                    under(hop, from_z)
            if 1 <= far <= nz:
                for hop in by_far[far - 1]:
                    under(hop, from_plane)
            if far >= 2:
                for hop in by_far[far - 2]:
                    under(hop, from_diagonal)
        for a in (0, 1):
            s.arrived((a, "c", 0))
        for hop in hops:
            under(hop, from_core)
        s.finish()

    cb_out, vw_out = call(
        kernel,
        [
            jax.ShapeDtypeStruct((nz, nx, CORES, nb, rows // nb, width), BF16),
            jax.ShapeDtypeStruct((nz, nx, CORES, nb, vrows // nb, bins), BF16),
        ],
        [pltpu.SemaphoreType.DMA((len(keys),)), pltpu.SemaphoreType.DMA((len(keys),))],
        1,
        codebook.reshape(nb, rows // nb, width),
        value_weight.reshape(nb, vrows // nb, bins),
    )
    return cb_out.reshape(nf * rows, width), vw_out.reshape(nf * vrows, bins)


def gather_grads(nb, nf, pre_grad, active, delta_t, value_delta):
    nz, nx = PLANES, nf // (PLANES * CORES)
    rows, width = pre_grad.shape
    bins = value_delta.shape[1]
    half = delta_t.shape[1]
    hops = [(0, 0)] + steps(nz)
    keys = [("c", 0)]
    for hop in hops:
        if hop[1]:
            keys += [("z", hop), ("cz", hop)]
        for dx in range(1, nx):
            keys += [("x", hop, dx), ("cx", hop, dx)]
    keys += [(k, dy) for dy in range(1, nb) for k in ("act", "delta", "value")]

    def kernel(pg, act, dt, vd, pg_out, act_out, dt_out, vd_out, send_sem, recv_sem):
        p = Place(nb, nf)
        p.barrier()
        s = Sends(send_sem, recv_sem, keys, p)
        here, like = pg_out.at[p.z, p.x, p.c], pg_out.at[0, 0, 0]
        mine = pl.ds(pl.multiple_of(p.b * rows, rows), rows)
        for way in (1, -1):

            @s.only(lambda way=way: feeds(p, way))
            def _(way=way):
                s.go(("z", (way, 1)), pg, here, p.dev(z=p.z + way), like)

        for dx in range(1, nx):
            s.go(("x", (0, 0), dx), pg, here, p.dev(x=p.xx(dx)))
        for dy in range(1, nb):
            to = p.bb(dy)
            s.go(("act", dy), act, act_out.at[p.b], p.dev(b=to))
            s.go(("delta", dy), dt.at[to], dt_out.at[:, mine], p.dev(b=to))
            s.go(("value", dy), vd, vd_out.at[p.b], p.dev(b=to))
        s.go(("c", 0), pg, here, p.dev(c=1 - p.c))
        pg_out[p.z, p.x, p.c] = pg[...]
        act_out[p.b] = act[...]
        dt_out[:, mine] = dt[p.b]
        vd_out[p.b] = vd[...]

        def from_z(hop):
            way, far = hop
            ref = pg_out.at[p.z - way * far, p.x, p.c]
            s.arrived(("z", hop))
            if far + 1 < nz:

                @s.only(lambda way=way: feeds(p, way))
                def _():
                    s.go(("z", (way, far + 1)), ref, ref, p.dev(z=p.z + way), like)

            for dx in range(1, nx):
                s.go(("x", hop, dx), ref, ref, p.dev(x=p.xx(dx)), like)
            s.go(("cz", hop), ref, ref, p.dev(c=1 - p.c), like)

        def from_plane(hop):
            way, far = hop
            for dx in range(1, nx):
                s.arrived(("x", hop, dx))
                ref = pg_out.at[p.z - way * far, p.xx(-dx), p.c]
                s.go(("cx", hop, dx), ref, ref, p.dev(c=1 - p.c), like)

        def from_core(hop):
            for key in keys:
                if key[0] in ("cz", "cx") and key[1] == hop:
                    s.arrived(key)

        def under(hop, f):
            if hop[1]:
                s.only(lambda: has(p, *hop))(lambda: f(hop))
            else:
                f(hop)

        for far in range(nz + 1):
            for hop in hops:
                if far and hop[1] == far:
                    under(hop, from_z)
            for hop in hops:
                if hop[1] == far - 1:
                    under(hop, from_plane)
        for key in keys:
            if key[0] in ("act", "delta", "value", "c"):
                s.arrived(key)
        for hop in hops:
            under(hop, from_core)
        s.finish()

    pieces, act_all, dt_all, vd_all = call(
        kernel,
        [
            jax.ShapeDtypeStruct((nz, nx, CORES, rows, width), BF16),
            jax.ShapeDtypeStruct((nb, rows, width), BF16),
            jax.ShapeDtypeStruct((half, nb * rows), BF16),
            jax.ShapeDtypeStruct((nb, rows, bins), BF16),
        ],
        [pltpu.SemaphoreType.DMA((len(keys),)), pltpu.SemaphoreType.DMA((len(keys),))],
        2,
        pre_grad,
        active,
        delta_t,
        value_delta,
    )
    return (
        pieces.reshape(nf * rows, width),
        act_all.reshape(nb * rows, width),
        dt_all,
        vd_all.reshape(nb * rows, bins),
    )


def reduce_grads(nb, nf, trunk, pieces, code, value):
    nz, nx = PLANES, nf // (PLANES * CORES)
    depth = trunk.shape[0]
    width = pieces.shape[1]
    block = next(n for n in (192, 96, 64, 32, 16) if depth % n == 0)
    blocks = depth // block
    lanes = 256
    cuts = 2 if code.shape[3] % 32 == 0 else 1
    crows, vrows = code.shape[3] // cuts, value.shape[4]
    bins = value.shape[5]
    chunks = range(cuts + 1)
    keys = [("p", i, dy) for i in range(blocks) for dy in range(1, nb)]
    for a in chunks:
        keys += [(a, "c")] + [(a, "x", d) for d in range(1, nx)]
        keys += [(a, "z", d) for d in range(1, nz)] + [(a, "y", d) for d in range(1, nb)]

    def kernel(tr, pg, cd, vl, pj_out, cd_out, vl_out, *rest):
        send_sem, recv_sem = rest[-2:]
        p = Place(nb, nf)
        p.barrier()
        s = Sends(send_sem, recv_sem, keys, p)
        arrays = []
        for a in chunks:
            if a < cuts:
                part = pl.ds(a * crows, crows)
                own, out = cd.at[:, :, :, part], cd_out.at[:, part]
            else:
                own, out = vl.at[:, :, :, p.b], vl_out
            arrays.append((a, own, out) + tuple(rest[6 * a : 6 * a + 6]))
        for a, own, out, core, *_ in arrays:
            s.go((a, "c"), own.at[:, :, 1 - p.c], core, p.dev(c=1 - p.c))

        def multiply(i):
            rows = pl.ds(i * block, block)

            def tile(n, carry):
                cols = pl.ds(pl.multiple_of(n * lanes, lanes), lanes)
                pj_out[p.b, rows, cols] = jnp.dot(
                    tr[rows, :], pg[:, cols], preferred_element_type=F32
                ).astype(BF16)
                return carry

            lax.fori_loop(0, width // lanes, tile, 0)
            for dy in range(1, nb):
                ref = pj_out.at[p.b, rows]
                s.go(("p", i, dy), ref, ref, p.dev(b=p.bb(dy)))

        multiply(0)
        for a, own, out, core, xin, xsend, acc, zin, zsend in arrays:
            s.arrived((a, "c"))
            for dx in range(1, nx):
                x = p.xx(dx)
                for z in range(nz):
                    both = own[z, x, p.c].astype(F32) + core[z, x].astype(F32)
                    xsend[dx - 1, z] = both.astype(BF16)
                s.go((a, "x", dx), xsend.at[dx - 1], xin.at[dx - 1], p.dev(x=x))
            for z in range(nz):
                acc[z] = own[z, p.x, p.c].astype(F32) + core[z, p.x].astype(F32)
        for i in range(1, blocks):
            multiply(i)
        for a, own, out, core, xin, xsend, acc, zin, zsend in arrays:
            for dx in range(1, nx):
                s.arrived((a, "x", dx))
                acc[...] += xin[dx - 1].astype(F32)
            for dz in [2, 1, 3]:
                z = p.zz(dz)
                zsend[dz - 1] = acc[z].astype(BF16)
                s.go((a, "z", dz), zsend.at[dz - 1], zin.at[dz - 1], p.dev(z=z))
        for a, own, out, core, xin, xsend, acc, zin, zsend in arrays:
            total = acc[p.z]
            for dz in range(1, nz):
                s.arrived((a, "z", dz))
                total = total + zin[dz - 1].astype(F32)
            out[p.b] = total.astype(BF16)
            for dy in range(1, nb):
                s.go((a, "y", dy), out.at[p.b], out.at[p.b], p.dev(b=p.bb(dy)))
        for key in keys:
            if key[0] == "p" or key[1] == "y":
                s.arrived(key)
        s.finish()

    def buffers(r, k):
        return [
            pltpu.VMEM((nz, nx, r, k), BF16),
            pltpu.VMEM((max(nx - 1, 1), nz, r, k), BF16),
            pltpu.VMEM((max(nx - 1, 1), nz, r, k), BF16),
            pltpu.VMEM((nz, r, k), F32),
            pltpu.VMEM((nz - 1, r, k), BF16),
            pltpu.VMEM((nz - 1, r, k), BF16),
        ]

    return call(
        kernel,
        [
            jax.ShapeDtypeStruct((nb, depth, width), BF16),
            jax.ShapeDtypeStruct((nb, crows * cuts, width), BF16),
            jax.ShapeDtypeStruct((nb, vrows, bins), BF16),
        ],
        buffers(crows, width) * cuts
        + buffers(vrows, bins)
        + [pltpu.SemaphoreType.DMA((len(keys),)), pltpu.SemaphoreType.DMA((len(keys),))],
        3,
        trunk,
        pieces,
        code,
        value,
    )


def make_body(nb, nf):
    nz, nx = PLANES, nf // (PLANES * CORES)

    def body(
        trunk, pre_act, proj_weight, codebook, value_weight, code_target, value_bin, value_frac
    ):
        all_codes, bins_weight = gather_weights(nb, nf, codebook, value_weight)
        rows, width = pre_act.shape
        num_codes = all_codes.shape[0]
        num_bins = bins_weight.shape[1]
        pre_value = pre_act.astype(F32)
        gate_sigma = jax.nn.sigmoid(pre_value)
        active = (pre_value * gate_sigma).astype(BF16)
        code_logits = jnp.einsum("rk,ck->rc", active, all_codes, preferred_element_type=F32)
        code_probs = jax.nn.softmax(code_logits, axis=-1)
        code_ids = lax.broadcasted_iota(jnp.int32, (1, num_codes), 1)
        one_hot = (code_target[:, None] == code_ids).astype(F32)
        code_delta = (code_probs - one_hot).astype(BF16)
        value_logits = jnp.dot(active, bins_weight, preferred_element_type=F32)
        value_probs = jax.nn.softmax(value_logits, axis=-1)
        bin_ids = lax.broadcasted_iota(jnp.int32, (1, num_bins), 1)
        fraction = value_frac.astype(F32)[:, None] / 1024.0
        target = jnp.where(bin_ids == value_bin[:, None], 1.0 - fraction, 0.0)
        target = target + jnp.where(bin_ids == value_bin[:, None] + 1, fraction, 0.0)
        value_delta = (value_probs - target).astype(BF16)
        backward = jnp.dot(code_delta, all_codes, preferred_element_type=F32)
        backward = backward + jnp.einsum(
            "rb,kb->rk", value_delta, bins_weight, preferred_element_type=F32
        )
        pre_grad = (backward * gate_sigma * (1.0 + pre_value * (1.0 - gate_sigma))).astype(BF16)
        own = codebook.shape[0] // nb
        delta_t = code_delta.T.reshape(nf, nb, own, rows).swapaxes(0, 1)
        delta_t = delta_t.reshape(nb, nf * own, rows)
        pieces, act_all, dt_all, vd_all = gather_grads(
            nb, nf, pre_grad, active, delta_t, value_delta
        )
        out_cols = jnp.einsum(
            "dk,rk->dr", proj_weight, pieces, preferred_element_type=F32
        ).astype(BF16)
        code_part = jnp.dot(dt_all, act_all, preferred_element_type=F32)
        code_part = code_part.astype(BF16).reshape(nz, nx, CORES, own, width)
        value_part = jnp.einsum("rk,rb->kb", act_all, vd_all, preferred_element_type=F32)
        vown = value_weight.shape[0] // nb
        value_part = value_part.astype(BF16).reshape(nz, nx, CORES, nb, vown, num_bins)
        proj_all, code_all, value_all = reduce_grads(nb, nf, trunk, pieces, code_part, value_part)
        proj_grad = jnp.sum(proj_all.astype(F32), axis=0)
        code_grad = code_all.reshape(nb * own, width).astype(F32)
        value_grad = value_all.reshape(nb * vown, num_bins).astype(F32)
        return (out_cols, proj_grad, code_grad, value_grad)

    return body


def solution(mesh):
    in_specs = (
        P("fsdp", "batch"),
        P(("batch", "fsdp"), None),
        P("fsdp", None),
        P("fsdp", None),
        P("fsdp", None),
        P(("batch", "fsdp")),
        P(("batch", "fsdp")),
        P(("batch", "fsdp")),
    )
    out_specs = (P("fsdp", "batch"), P("fsdp", None), P("fsdp", None), P("fsdp", None))
    body = make_body(mesh.shape["batch"], mesh.shape["fsdp"])
    return jax.shard_map(body, mesh=mesh, in_specs=in_specs, out_specs=out_specs, check_vma=False)
```

```python
import jax
import jax.numpy as jnp
from jax import lax
from jax.experimental import pallas as pl
from jax.experimental.pallas import tpu as pltpu
from jax.sharding import PartitionSpec as P

MESH = pl.DeviceIdType.MESH
BF16 = jnp.bfloat16
F32 = jnp.float32
CORES = 2
PLANES = 4


class Place:
    def __init__(self, nb, nf):
        self.nb, self.nz = nb, PLANES
        self.nx = nf // (PLANES * CORES)
        f = lax.axis_index("fsdp")
        self.b = lax.axis_index("batch")
        self.z = f // (self.nx * CORES)
        self.x = (f // CORES) % self.nx
        self.c = f % CORES

    def dev(self, b=None, z=None, x=None, c=None):
        b = self.b if b is None else b
        z = self.z if z is None else z
        x = self.x if x is None else x
        c = self.c if c is None else c
        return (b, (z * self.nx + x) * CORES + c)

    def zz(self, d):
        return lax.rem(self.z + d + self.nz, self.nz)

    def xx(self, d):
        return lax.rem(self.x + d + self.nx, self.nx)

    def bb(self, d):
        return lax.rem(self.b + d + self.nb, self.nb)

    def barrier(self):
        sem = pltpu.get_barrier_semaphore()
        peers = [self.dev(z=self.zz(d)) for d in range(1, self.nz)]
        peers += [self.dev(x=self.xx(d)) for d in range(1, self.nx)]
        peers += [self.dev(b=self.bb(d)) for d in range(1, self.nb)]
        peers += [self.dev(c=1 - self.c)]
        for peer in peers:
            pl.semaphore_signal(sem, inc=1, device_id=peer, device_id_type=MESH)
        pl.semaphore_wait(sem, len(peers))


def steps(nz):
    return [(way, far) for far in range(1, nz) for way in (1, -1)]


class Sends:
    def __init__(self, send_sem, recv_sem, keys, place):
        self.send_sem, self.recv_sem, self.place = send_sem, recv_sem, place
        self.at = {k: i for i, k in enumerate(keys)}
        self.like = {}
        self.started = []
        self.when = ()

    def make(self, key, src, dst, dev):
        i = self.at[key]
        return pltpu.make_async_remote_copy(
            src_ref=src,
            dst_ref=dst,
            send_sem=self.send_sem.at[i],
            recv_sem=self.recv_sem.at[i],
            device_id=dev,
            device_id_type=MESH,
        )

    def go(self, key, src, dst, dev, like=None):
        self.make(key, src, dst, dev).start()
        self.like[key] = dst if like is None else like
        self.started.append((key, self.when))

    def waiter(self, key):
        ref = self.like[key]
        ref = ref() if callable(ref) else ref
        return self.make(key, ref, ref, self.place.dev(c=1 - self.place.c))

    def arrived(self, key):
        self.waiter(key).wait_recv()

    def finish(self):
        for key, whens in self.started:

            def wait(key=key):
                self.waiter(key).wait_send()

            if whens:
                met = whens[0]()
                for when in whens[1:]:
                    met = jnp.logical_and(met, when())
                pl.when(met)(wait)
            else:
                wait()

    def only(self, when):
        def run(f):
            outer = self.when
            self.when = outer + (when,)

            @pl.when(when())
            def _():
                f()

            self.when = outer

        return run


def call(kernel, outs, scratch, cid, *args):
    return pl.pallas_call(
        kernel,
        out_shape=outs,
        in_specs=[pl.BlockSpec(memory_space=pltpu.VMEM)] * len(args),
        out_specs=[pl.BlockSpec(memory_space=pltpu.VMEM)] * len(outs),
        scratch_shapes=scratch,
        compiler_params=pltpu.CompilerParams(collective_id=cid, has_side_effects=True),
    )(*args)


def has(p, way, far):
    return p.z >= far if way == 1 else p.z + far < p.nz


def feeds(p, way):
    return p.z + 1 < p.nz if way == 1 else p.z >= 1


def gather_weights_keys(nb, nx, nz):
    keys = []
    for a in (0, 1):
        keys += [(a, "c", 0)]
        for hop in [(0, 0)] + steps(nz):
            if hop[1]:
                keys += [(a, "z", hop), (a, "cz", hop)]
                for dy in range(1, nb):
                    keys += [(a, "y", hop, dy), (a, "cy", hop, dy)]
            for dx in range(1, nx):
                keys += [(a, "x", hop, dx), (a, "cx", hop, dx)]
                for dy in range(1, nb):
                    keys += [(a, "d", hop, dx, dy), (a, "cd", hop, dx, dy)]
    return keys


def gather_weights(nb, nf, codebook, value_weight):
    nz, nx = PLANES, nf // (PLANES * CORES)
    keys = gather_weights_keys(nb, nx, nz)
    rows, width = codebook.shape
    vrows, bins = value_weight.shape

    def kernel(cb, vw, cb_out, vw_out, send_sem, recv_sem):
        p = Place(nb, nf)
        p.barrier()
        s = Sends(send_sem, recv_sem, keys, p)
        arrays = ((0, cb, cb_out), (1, vw, vw_out))

        def spot(out, z, x, h):
            return out.at[z, x, p.c, h]

        def relay(key, out, at_z, at_x, at_h, **to):
            ref = spot(out, at_z, at_x, at_h)
            s.go(key, ref, ref, p.dev(**to), lambda: out.at[0, 0, 0, 0])

        for a, own, out in arrays:
            here = spot(out, p.z, p.x, p.b)
            for way in (1, -1):

                @s.only(lambda way=way: feeds(p, way))
                def _(a=a, own=own, out=out, here=here, way=way):
                    s.go((a, "z", (way, 1)), own.at[p.b], here, p.dev(z=p.z + way), lambda: out.at[0, 0, 0, 0])

            for dx in range(1, nx):
                s.go((a, "x", (0, 0), dx), own.at[p.b], here, p.dev(x=p.xx(dx)))
            s.go((a, "c", 0), own, out.at[p.z, p.x, p.c], p.dev(c=1 - p.c))
        for a, own, out in arrays:
            out[p.z, p.x, p.c] = own[...]

        def from_z(hop):
            way, far = hop
            z = p.z - way * far
            for a, own, out in arrays:
                s.arrived((a, "z", hop))
                if far + 1 < nz:

                    @s.only(lambda way=way: feeds(p, way))
                    def _(a=a, out=out):
                        relay((a, "z", (way, far + 1)), out, z, p.x, p.b, z=p.z + way)

                for dx in range(1, nx):
                    relay((a, "x", hop, dx), out, z, p.x, p.b, x=p.xx(dx))
                for dy in range(1, nb):
                    relay((a, "y", hop, dy), out, z, p.x, p.b, b=p.bb(dy))
                relay((a, "cz", hop), out, z, p.x, p.b, c=1 - p.c)

        def from_plane(hop):
            way, far = hop
            z = p.z - way * far
            for a, own, out in arrays:
                for dx in range(1, nx):
                    x = p.xx(-dx)
                    s.arrived((a, "x", hop, dx))
                    if far % 2 == 0:
                        for dy in range(1, nb):
                            relay((a, "d", hop, dx, dy), out, z, x, p.b, b=p.bb(dy))
                    relay((a, "cx", hop, dx), out, z, x, p.b, c=1 - p.c)
                if far:
                    for dy in range(1, nb):
                        h = p.bb(-dy)
                        s.arrived((a, "y", hop, dy))
                        if far % 2:
                            for dx in range(1, nx):
                                relay((a, "d", hop, dx, dy), out, z, p.x, h, x=p.xx(dx))
                        relay((a, "cy", hop, dy), out, z, p.x, h, c=1 - p.c)

        def from_diagonal(hop):
            way, far = hop
            for a, own, out in arrays:
                for dx in range(1, nx):
                    for dy in range(1, nb):
                        s.arrived((a, "d", hop, dx, dy))
                        relay(
                            (a, "cd", hop, dx, dy),
                            out,
                            p.z - way * far,
                            p.xx(-dx),
                            p.bb(-dy),
                            c=1 - p.c,
                        )

        def from_core(hop):
            for key in keys:
                if key[1] in ("cz", "cx", "cy", "cd") and key[2] == hop:
                    s.arrived(key)

        def under(hop, f):
            if hop[1]:
                s.only(lambda: has(p, *hop))(lambda: f(hop))
            else:
                f(hop)

        hops = [(0, 0)] + steps(nz)
        by_far = [[h for h in hops if h[1] == far] for far in range(nz)]
        for far in range(nz + 2):
            if 1 <= far < nz:
                for hop in by_far[far]:
                    under(hop, from_z)
            if 1 <= far <= nz:
                for hop in by_far[far - 1]:
                    under(hop, from_plane)
            if far >= 2:
                for hop in by_far[far - 2]:
                    under(hop, from_diagonal)
        for a in (0, 1):
            s.arrived((a, "c", 0))
        for hop in hops:
            under(hop, from_core)
        s.finish()

    cb_out, vw_out = call(
        kernel,
        [
            jax.ShapeDtypeStruct((nz, nx, CORES, nb, rows // nb, width), BF16),
            jax.ShapeDtypeStruct((nz, nx, CORES, nb, vrows // nb, bins), BF16),
        ],
        [pltpu.SemaphoreType.DMA((len(keys),)), pltpu.SemaphoreType.DMA((len(keys),))],
        1,
        codebook.reshape(nb, rows // nb, width),
        value_weight.reshape(nb, vrows // nb, bins),
    )
    return cb_out.reshape(nf * rows, width), vw_out.reshape(nf * vrows, bins)


def gather_grads(nb, nf, pre_grad, active, delta_t, value_delta):
    nz, nx = PLANES, nf // (PLANES * CORES)
    rows, width = pre_grad.shape
    bins = value_delta.shape[1]
    half = delta_t.shape[1]
    hops = [(0, 0)] + steps(nz)
    keys = [("c", 0)]
    for hop in hops:
        if hop[1]:
            keys += [("z", hop), ("cz", hop)]
        for dx in range(1, nx):
            keys += [("x", hop, dx), ("cx", hop, dx)]
    keys += [(k, dy) for dy in range(1, nb) for k in ("act", "delta", "value")]

    def kernel(pg, act, dt, vd, pg_out, act_out, dt_out, vd_out, send_sem, recv_sem):
        p = Place(nb, nf)
        p.barrier()
        s = Sends(send_sem, recv_sem, keys, p)
        here, like = pg_out.at[p.z, p.x, p.c], pg_out.at[0, 0, 0]
        mine = pl.ds(pl.multiple_of(p.b * rows, rows), rows)
        for way in (1, -1):

            @s.only(lambda way=way: feeds(p, way))
            def _(way=way):
                s.go(("z", (way, 1)), pg, here, p.dev(z=p.z + way), like)

        for dx in range(1, nx):
            s.go(("x", (0, 0), dx), pg, here, p.dev(x=p.xx(dx)))
        for dy in range(1, nb):
            to = p.bb(dy)
            s.go(("act", dy), act, act_out.at[p.b], p.dev(b=to))
            s.go(("delta", dy), dt.at[to], dt_out.at[:, mine], p.dev(b=to))
            s.go(("value", dy), vd, vd_out.at[p.b], p.dev(b=to))
        s.go(("c", 0), pg, here, p.dev(c=1 - p.c))
        pg_out[p.z, p.x, p.c] = pg[...]
        act_out[p.b] = act[...]
        dt_out[:, mine] = dt[p.b]
        vd_out[p.b] = vd[...]

        def from_z(hop):
            way, far = hop
            ref = pg_out.at[p.z - way * far, p.x, p.c]
            s.arrived(("z", hop))
            if far + 1 < nz:

                @s.only(lambda way=way: feeds(p, way))
                def _():
                    s.go(("z", (way, far + 1)), ref, ref, p.dev(z=p.z + way), like)

            for dx in range(1, nx):
                s.go(("x", hop, dx), ref, ref, p.dev(x=p.xx(dx)), like)
            s.go(("cz", hop), ref, ref, p.dev(c=1 - p.c), like)

        def from_plane(hop):
            way, far = hop
            for dx in range(1, nx):
                s.arrived(("x", hop, dx))
                ref = pg_out.at[p.z - way * far, p.xx(-dx), p.c]
                s.go(("cx", hop, dx), ref, ref, p.dev(c=1 - p.c), like)

        def from_core(hop):
            for key in keys:
                if key[0] in ("cz", "cx") and key[1] == hop:
                    s.arrived(key)

        def under(hop, f):
            if hop[1]:
                s.only(lambda: has(p, *hop))(lambda: f(hop))
            else:
                f(hop)

        for far in range(nz + 1):
            for hop in hops:
                if far and hop[1] == far:
                    under(hop, from_z)
            for hop in hops:
                if hop[1] == far - 1:
                    under(hop, from_plane)
        for key in keys:
            if key[0] in ("act", "delta", "value", "c"):
                s.arrived(key)
        for hop in hops:
            under(hop, from_core)
        s.finish()

    pieces, act_all, dt_all, vd_all = call(
        kernel,
        [
            jax.ShapeDtypeStruct((nz, nx, CORES, rows, width), BF16),
            jax.ShapeDtypeStruct((nb, rows, width), BF16),
            jax.ShapeDtypeStruct((half, nb * rows), BF16),
            jax.ShapeDtypeStruct((nb, rows, bins), BF16),
        ],
        [pltpu.SemaphoreType.DMA((len(keys),)), pltpu.SemaphoreType.DMA((len(keys),))],
        2,
        pre_grad,
        active,
        delta_t,
        value_delta,
    )
    return (
        pieces.reshape(nf * rows, width),
        act_all.reshape(nb * rows, width),
        dt_all,
        vd_all.reshape(nb * rows, bins),
    )


def reduce_grads(nb, nf, trunk, proj_weight, pieces, code, value):
    nz, nx = PLANES, nf // (PLANES * CORES)
    depth = trunk.shape[0]
    width = pieces.shape[1]
    block = next(n for n in (192, 96, 64, 32, 16) if depth % n == 0)
    blocks = depth // block
    lanes = 256
    cuts = 2 if code.shape[3] % 32 == 0 else 1
    crows = code.shape[3] // cuts
    fused = len(value) == 2
    bins = value[-1].shape[-1]
    vrows = width // (nf * nb) if fused else value[0].shape[4]
    chunks = range(cuts + 1)
    keys = [("p", i, dy) for i in range(blocks) for dy in range(1, nb)]
    for a in chunks:
        keys += [(a, "c")] + [(a, "x", d) for d in range(1, nx)]
        keys += [(a, "z", d) for d in range(1, nz)] + [(a, "y", d) for d in range(1, nb)]

    def kernel(tr, pw, pg, cd, *rest):
        factors, rest = rest[: len(value)], rest[len(value) :]
        (tr_out, pj_out, cd_out, vl_out), rest = rest[:4], rest[4:]
        send_sem, recv_sem = rest[-2:]
        vl = rest[-3] if fused else factors[0]
        p = Place(nb, nf)
        p.barrier()
        s = Sends(send_sem, recv_sem, keys, p)
        arrays = []
        for a in chunks:
            if a < cuts:
                part = pl.ds(a * crows, crows)
                own, out = cd.at[:, :, :, part], cd_out.at[:, part]
            else:
                own, out = vl.at[:, :, :, p.b], vl_out
            arrays.append((a, own, out) + tuple(rest[6 * a : 6 * a + 6]))
        for a, own, out, core, *_ in arrays:
            if a == cuts and fused:
                product = lax.dot_general(
                    factors[0][...],
                    factors[1][...],
                    (((0,), (0,)), ((), ())),
                    preferred_element_type=F32,
                )
                vl[...] = product.astype(BF16).reshape(nz, nx, CORES, nb, vrows, bins)
            s.go((a, "c"), own.at[:, :, 1 - p.c], core, p.dev(c=1 - p.c))

        def multiply(i):
            rows = pl.ds(i * block, block)

            def tile(n, carry):
                cols = pl.ds(pl.multiple_of(n * lanes, lanes), lanes)
                pj_out[p.b, rows, cols] = jnp.dot(
                    tr[rows, :], pg[:, cols], preferred_element_type=F32
                ).astype(BF16)
                return carry

            lax.fori_loop(0, width // lanes, tile, 0)
            for dy in range(1, nb):
                ref = pj_out.at[p.b, rows]
                s.go(("p", i, dy), ref, ref, p.dev(b=p.bb(dy)))

        def columns(n, carry):
            cols = pl.ds(pl.multiple_of(n * lanes, lanes), lanes)
            tr_out[:, cols] = lax.dot_general(
                pw[...], pg[cols, :], (((1,), (1,)), ((), ())), preferred_element_type=F32
            ).astype(BF16)
            return carry

        multiply(0)
        for a, own, out, core, xin, xsend, acc, zin, zsend in arrays:
            s.arrived((a, "c"))
            for dx in range(1, nx):
                x = p.xx(dx)
                for z in range(nz):
                    both = own[z, x, p.c].astype(F32) + core[z, x].astype(F32)
                    xsend[dx - 1, z] = both.astype(BF16)
                s.go((a, "x", dx), xsend.at[dx - 1], xin.at[dx - 1], p.dev(x=x))
            for z in range(nz):
                acc[z] = own[z, p.x, p.c].astype(F32) + core[z, p.x].astype(F32)
        for i in range(1, blocks):
            multiply(i)
        for a, own, out, core, xin, xsend, acc, zin, zsend in arrays:
            for dx in range(1, nx):
                s.arrived((a, "x", dx))
                acc[...] += xin[dx - 1].astype(F32)
            for dz in [2, 1, 3]:
                z = p.zz(dz)
                zsend[dz - 1] = acc[z].astype(BF16)
                s.go((a, "z", dz), zsend.at[dz - 1], zin.at[dz - 1], p.dev(z=z))
        for a, own, out, core, xin, xsend, acc, zin, zsend in arrays:
            if a == 0:
                lax.fori_loop(0, pieces.shape[0] // lanes, columns, 0)
            total = acc[p.z]
            for dz in range(1, nz):
                s.arrived((a, "z", dz))
                total = total + zin[dz - 1].astype(F32)
            out[p.b] = total.astype(BF16)
            for dy in range(1, nb):
                s.go((a, "y", dy), out.at[p.b], out.at[p.b], p.dev(b=p.bb(dy)))
        for key in keys:
            if key[0] == "p" or key[1] == "y":
                s.arrived(key)
        s.finish()

    def buffers(r, k):
        return [
            pltpu.VMEM((nz, nx, r, k), BF16),
            pltpu.VMEM((max(nx - 1, 1), nz, r, k), BF16),
            pltpu.VMEM((max(nx - 1, 1), nz, r, k), BF16),
            pltpu.VMEM((nz, r, k), F32),
            pltpu.VMEM((nz - 1, r, k), BF16),
            pltpu.VMEM((nz - 1, r, k), BF16),
        ]

    return call(
        kernel,
        [
            jax.ShapeDtypeStruct((depth, pieces.shape[0]), BF16),
            jax.ShapeDtypeStruct((nb, depth, width), BF16),
            jax.ShapeDtypeStruct((nb, crows * cuts, width), BF16),
            jax.ShapeDtypeStruct((nb, vrows, bins), BF16),
        ],
        buffers(crows, width) * cuts
        + buffers(vrows, bins)
        + [pltpu.VMEM((nz, nx, CORES, nb, vrows, bins), BF16)] * fused
        + [pltpu.SemaphoreType.DMA((len(keys),)), pltpu.SemaphoreType.DMA((len(keys),))],
        3,
        trunk,
        proj_weight,
        pieces,
        code,
        *value,
    )


def make_body(nb, nf):
    nz, nx = PLANES, nf // (PLANES * CORES)

    def body(
        trunk, pre_act, proj_weight, codebook, value_weight, code_target, value_bin, value_frac
    ):
        all_codes, bins_weight = gather_weights(nb, nf, codebook, value_weight)
        rows, width = pre_act.shape
        num_codes = all_codes.shape[0]
        num_bins = bins_weight.shape[1]
        pre_value = pre_act.astype(F32)
        gate_sigma = jax.nn.sigmoid(pre_value)
        active = (pre_value * gate_sigma).astype(BF16)
        code_logits = jnp.einsum("rk,ck->rc", active, all_codes, preferred_element_type=F32)
        code_probs = jax.nn.softmax(code_logits, axis=-1)
        code_ids = lax.broadcasted_iota(jnp.int32, (1, num_codes), 1)
        one_hot = (code_target[:, None] == code_ids).astype(F32)
        code_delta = (code_probs - one_hot).astype(BF16)
        value_logits = jnp.dot(active, bins_weight, preferred_element_type=F32)
        value_probs = jax.nn.softmax(value_logits, axis=-1)
        bin_ids = lax.broadcasted_iota(jnp.int32, (1, num_bins), 1)
        fraction = value_frac.astype(F32)[:, None] / 1024.0
        target = jnp.where(bin_ids == value_bin[:, None], 1.0 - fraction, 0.0)
        target = target + jnp.where(bin_ids == value_bin[:, None] + 1, fraction, 0.0)
        value_delta = (value_probs - target).astype(BF16)
        backward = jnp.dot(code_delta, all_codes, preferred_element_type=F32)
        backward = backward + jnp.einsum(
            "rb,kb->rk", value_delta, bins_weight, preferred_element_type=F32
        )
        pre_grad = (backward * gate_sigma * (1.0 + pre_value * (1.0 - gate_sigma))).astype(BF16)
        own = codebook.shape[0] // nb
        delta_t = code_delta.T.reshape(nf, nb, own, rows).swapaxes(0, 1)
        delta_t = delta_t.reshape(nb, nf * own, rows)
        pieces, act_all, dt_all, vd_all = gather_grads(
            nb, nf, pre_grad, active, delta_t, value_delta
        )
        code_part = jnp.dot(dt_all, act_all, preferred_element_type=F32)
        code_part = code_part.astype(BF16).reshape(nz, nx, CORES, own, width)
        vown = value_weight.shape[0] // nb
        if vown % 16 == 0:
            value_part = (act_all, vd_all)
        else:
            value_part = jnp.einsum("rk,rb->kb", act_all, vd_all, preferred_element_type=F32)
            value_part = value_part.astype(BF16)
            value_part = (value_part.reshape(nz, nx, CORES, nb, vown, num_bins),)
        out_cols, proj_all, code_all, value_all = reduce_grads(
            nb, nf, trunk, proj_weight, pieces, code_part, value_part
        )
        proj_grad = jnp.sum(proj_all.astype(F32), axis=0)
        code_grad = code_all.reshape(nb * own, width).astype(F32)
        value_grad = value_all.reshape(nb * vown, num_bins).astype(F32)
        return (out_cols, proj_grad, code_grad, value_grad)

    return body


def solution(mesh):
    in_specs = (
        P("fsdp", "batch"),
        P(("batch", "fsdp"), None),
        P("fsdp", None),
        P("fsdp", None),
        P("fsdp", None),
        P(("batch", "fsdp")),
        P(("batch", "fsdp")),
        P(("batch", "fsdp")),
    )
    out_specs = (P("fsdp", "batch"), P("fsdp", None), P("fsdp", None), P("fsdp", None))
    body = make_body(mesh.shape["batch"], mesh.shape["fsdp"])
    return jax.shard_map(body, mesh=mesh, in_specs=in_specs, out_specs=out_specs, check_vma=False)
```
